32 devices in a mesh: groups: 2 (over x), angle: 8 (over z, y), tile: 2 (over core).
Axes of the slice: x: 2, y: 2, z: 4, core: 2. Of those that a mesh axis runs over, the one named last changes fastest.
Arguments:
- intensity: float32 [128, 128, 2048], P(('groups', 'angle', 'tile')), parts along dimension 0, may hold values from 0.2 to 1
- counts: int32 [16], P('groups'), parts along dimension 0, may hold values from 1 to 32, 128 in all
- segment_ids: int32 [64, 64], replicated, may hold values from 0 to 15
- tile_ids: int32 [64, 64], replicated, may hold values from 0 to 15
- block_order: int32 [128], P('groups'), parts along dimension 0, may hold values from 0 to 63, each once
- tiles: bfloat16 [16, 128, 128], replicated, may hold values from -0.0625 to 0.0625
Outputs:
- volume: float32 [16, 32, 64, 128], P(('groups', 'angle'), None, 'tile'), parts along dimension 0
The draws below stay inside these ranges and needn't reach their ends.
There are 2 independent parts, one for each index of `groups`. The reference program is written for one: setup_inputs(seed, part) draws one part's arguments, and reference() takes and returns one part's arrays. A program takes and returns all parts, laid end to end along the dimension named above; an argument that names none is the same for every part. Nothing has to cross between parts.
Inputs may be any that keep to these rules, and one draw needn't show every extreme that they name: Slice group g takes counts[g] consecutive detector rows, groups in order; the counts sum to 128 and the largest is exactly 32. `block_order`: each voxel block appears once.
All inputs are finite; a program needn't handle non-finite values.
Results may differ from the reference program's by a relative error of at most 0.00075.
Values may be sent and summed in bfloat16 or wider, within the bound.
No kernel may reach another device: no remote copies, remote signals or barrier semaphores. Data moves between devices by JAX's collectives and lax.ppermute only.
A program may use at most 128 MiB of HBM per device.

```python
import math
import jax
import jax.numpy as jnp
import numpy as np
from jax import lax

ROWS = 128
W = 2048
VOX = 128
NT = 16
ANGLES = 64
GMAX = 32
NB = 64
SEGS = 16
N_ANGLE = 8


def touch_ends(result, rng, low, largest):
    place = [jax.random.randint(jax.random.fold_in(rng, axis), (), 0, length) for axis, length in enumerate(result.shape)]
    main_axis = result.shape.index(max(result.shape))
    next_to = place[:main_axis] + [(place[main_axis] + 1) % result.shape[main_axis]] + place[main_axis + 1:]
    return result.at[tuple(place)].set(low).at[tuple(next_to)].set(largest)


def level_of(rng, shape, cuts, least, largest):
    def one(axis_at, shards_of):
        steps = jax.random.uniform(jax.random.fold_in(jax.random.fold_in(rng, 6), axis_at), (shards_of,), jnp.float32, least / len(cuts), largest / len(cuts))
        return jnp.repeat(jnp.exp(steps), shape[axis_at] // shards_of).reshape((-1,) + (1,) * (len(shape) - axis_at - 1))

    gain = one(*cuts[0])
    for cut in cuts[1:]:
        gain = gain * one(*cut)
    return gain


def split_up(number_of, total, reach, lean):
    weights = [(1 << 20) // math.isqrt(grade ** lean) + 1 for grade in range(2, number_of + 1)]
    spare, given = total - reach - (number_of - 1), [1] * (number_of - 1)
    while spare > 0:
        candidates = [i for i in range(number_of - 1) if given[i] < reach]
        pool, left = sum([weights[i] for i in candidates]), spare
        for i in candidates:
            addition = min(reach - given[i], max(1, left * weights[i] // pool), spare)
            given[i] = given[i] + addition
            spare = spare - addition
    return np.array([reach] + given)


def ragged_sizes(stream_key, count, total, most, lean):
    if count == 2:
        one = jax.random.randint(stream_key, (), max(1, total - most), min(most, total - 1) + 1)
        return jnp.stack([one, total - one])
    sizes = jnp.asarray(split_up(count, total, most, lean), jnp.int32)
    couples = (count - 1) // 2
    donor, taker = sizes[1:1 + 2 * couples:2], sizes[2:2 + 2 * couples:2]
    slack = jnp.minimum(donor - 1, most - taker)
    passed = jax.random.randint(jax.random.fold_in(stream_key, 1), (couples,), 0, 1 << 20) % (slack + 1)
    sizes = sizes.at[1:1 + 2 * couples:2].set(donor - passed).at[2:2 + 2 * couples:2].set(taker + passed)
    return sizes[jax.random.permutation(jax.random.fold_in(stream_key, 2), count)]


def centred(key, extent, spread, limit, kind=jnp.bfloat16):
    return jnp.clip(spread * jax.random.normal(key, extent, jnp.float32), -limit, limit).astype(kind)


def setup_inputs(seed: int = 0, part: int = 0) -> dict:
    key_of = jax.random.split(jax.random.key(seed), 7)
    part_keys = jax.random.split(jax.random.fold_in(key_of[6], part), 7)
    intensity = jnp.clip(0.2 + 0.8 * jax.random.uniform(part_keys[0], (ANGLES, ROWS, W), jnp.float32) ** level_of(part_keys[0], (ANGLES, ROWS, W), ((0, 16),), -0.2, 0.2), 0.2, 1.0)
    counts = ragged_sizes(part_keys[1], N_ANGLE, ROWS, GMAX, 2).astype(jnp.int32)
    segment_ids = touch_ends(jax.random.randint(key_of[2], (ANGLES, NB), 0, SEGS), jax.random.fold_in(key_of[2], 1), 0, SEGS - 1).astype(jnp.int32)
    tile_ids = touch_ends(jax.random.randint(key_of[3], (ANGLES, NB), 0, NT), jax.random.fold_in(key_of[3], 1), 0, NT - 1).astype(jnp.int32)
    block_order = jax.random.permutation(part_keys[4], NB).astype(jnp.int32)
    tiles = centred(key_of[5], (NT, VOX, VOX), (VOX * ANGLES) ** -0.5, 0.0625)
    return {"intensity": intensity, "counts": counts, "segment_ids": segment_ids, "tile_ids": tile_ids, "block_order": block_order, "tiles": tiles}


paganin_alpha = 2.0


def reference(intensity, counts, segment_ids, tile_ids, block_order, tiles):
    row_freq = jnp.arange(ROWS).astype(jnp.float32)
    col_freq = jnp.arange(W).astype(jnp.float32)
    row_weight = 4.0 * jnp.square(jnp.sin(jnp.pi * row_freq / ROWS))
    col_weight = 4.0 * jnp.square(jnp.sin(jnp.pi * col_freq / W))
    weight = 1.0 / (1.0 + paganin_alpha * (row_weight[:, None] + col_weight[None, :]))

    def filter_one(projection):
        spectrum = jnp.fft.fft2(projection)
        return jnp.real(jnp.fft.ifft2(spectrum * weight))

    filtered = lax.map(filter_one, intensity)
    thickness = (-jnp.log(filtered)).astype(jnp.bfloat16)
    seg_ordered = jnp.take(segment_ids, block_order, axis=1)
    tile_ordered = jnp.take(tile_ids, block_order, axis=1)
    onehot = (tile_ordered[:, :, None] == jnp.arange(NT, dtype=jnp.int32)[None, None, :]).astype(jnp.float32)
    tiles_wide = tiles.astype(jnp.float32)

    def one_row(row_slices):
        pieces = row_slices.astype(jnp.float32).reshape(ANGLES, W // VOX, VOX)
        chosen = jnp.take_along_axis(pieces, seg_ordered[:, :, None], axis=1)
        grouped = jnp.einsum('avc,avx->vcx', onehot, chosen, precision=lax.Precision.HIGHEST)
        return jnp.einsum('vcx,cxy->vy', grouped, tiles_wide, precision=lax.Precision.HIGHEST)

    voxel_rows = lax.map(one_row, jnp.swapaxes(thickness, 0, 1))
    starts = (jnp.cumsum(counts) - counts).astype(jnp.int32)
    slot_index = jnp.arange(GMAX, dtype=jnp.int32)
    row_index = jnp.minimum(starts[:, None] + slot_index[None, :], ROWS - 1).astype(jnp.int32)
    slot_valid = slot_index[None, :] < counts[:, None]
    gathered = jnp.take(voxel_rows, row_index.reshape(-1), axis=0).reshape(N_ANGLE, GMAX, NB, VOX)
    return jnp.where(slot_valid[:, :, None, None], gathered, jnp.zeros((), jnp.float32))
```

```python
import functools
import math

import jax
import jax.numpy as jnp
import numpy as np
from jax import lax
from jax.experimental import pallas as pl
from jax.experimental.pallas import tpu as pltpu
from jax.sharding import PartitionSpec as P

paganin_alpha = 2.0
lanes = 128
thickness_bound = 1.75
send_bound = 60000.0


def split_parts(values):
    high = values.astype(jnp.bfloat16)
    low = (values - high.astype(jnp.float32)).astype(jnp.bfloat16)
    return high, low


def split_table(matrix):
    high = matrix.astype(jnp.bfloat16)
    low = (matrix - high.astype(np.float64)).astype(jnp.bfloat16)
    top = np.concatenate([high, high], axis=1)
    bottom = np.concatenate([low, low], axis=1)
    return jnp.asarray(np.concatenate([top, bottom], axis=0))


def filter_tables(row_total, width):
    levels = width.bit_length() - 1
    assert 1 << levels == width
    index = np.arange(row_total)
    phase = 2.0 * np.pi / row_total * (index[:, None] * index[None, :] % row_total)
    hartley = (np.cos(phase) + np.sin(phase)) / math.sqrt(row_total)
    row_weight = 4.0 * np.square(np.sin(np.pi * index / row_total))
    half = (1.0 + paganin_alpha * (row_weight + 2.0)) / (2.0 * paganin_alpha)
    root = half - np.sqrt(half * half - 1.0)
    scale = root / paganin_alpha / np.square(1.0 - root**width)
    factors = np.zeros((row_total, lanes), np.float32)
    for s in range(levels):
        power = root ** (1 << s)
        factors[:, s] = power / (1.0 + power * power)
        scale = scale * (1.0 + power * power)
    return split_table(hartley), split_table(hartley * scale[None, :]), jnp.asarray(factors)


def shifted(values, distance):
    width = values.shape[1]
    if distance % lanes:
        return pltpu.roll(values, distance, 1)
    return jnp.concatenate([values[:, width - distance :], values[:, : width - distance]], axis=1)


def filter_kernel(forward_ref, back_ref, factor_ref, f_ref, out_ref, modes_ref, parts_ref):
    row_total, width = f_ref.shape[1:]
    levels = width.bit_length() - 1
    high, low = split_parts(f_ref[0])
    parts_ref[:row_total] = high
    parts_ref[row_total:] = low
    both = jnp.dot(forward_ref[...], parts_ref[...], preferred_element_type=jnp.float32)
    modes_ref[...] = both[:row_total] + both[row_total:]

    def column_filter(step, carry):
        pieces = []
        for half in range(2):
            rows = pl.ds(pl.multiple_of(step * 16 + half * 8, 8), 8)
            values = modes_ref[rows, :]
            factors = factor_ref[rows, :]
            for s in range(levels):
                distance = 1 << s
                around = shifted(values, distance) + shifted(values, width - distance)
                values = values + factors[:, s : s + 1] * around
            pieces.append(values)
        high, low = split_parts(jnp.concatenate(pieces, axis=0))
        parts_ref[pl.ds(pl.multiple_of(step * 16, 16), 16), :] = high
        parts_ref[pl.ds(pl.multiple_of(row_total + step * 16, 16), 16), :] = low
        return carry

    lax.fori_loop(0, row_total // 16, column_filter, 0)
    both = jnp.dot(back_ref[...], parts_ref[...], preferred_element_type=jnp.float32)
    thickness = (-jnp.log(both[:row_total] + both[row_total:])).astype(jnp.bfloat16)
    edge = out_ref.shape[3]
    for segment in range(width // edge):
        out_ref[0, segment] = thickness[:, segment * edge : (segment + 1) * edge]


def paganin_thickness(intensity, voxel_edge):
    angle_count, row_total, width = intensity.shape
    forward, back, factors = filter_tables(row_total, width)
    segments = width // voxel_edge
    whole = lambda a: (0, 0)
    return pl.pallas_call(
        filter_kernel,
        grid=(angle_count,),
        in_specs=[
            pl.BlockSpec(forward.shape, whole),
            pl.BlockSpec(back.shape, whole),
            pl.BlockSpec(factors.shape, whole),
            pl.BlockSpec((1, row_total, width), lambda a: (a, 0, 0)),
        ],
        out_specs=pl.BlockSpec((1, segments, row_total, voxel_edge), lambda a: (a, 0, 0, 0)),
        out_shape=jax.ShapeDtypeStruct((angle_count, segments, row_total, voxel_edge), jnp.bfloat16),
        scratch_shapes=[
            pltpu.VMEM((row_total, width), jnp.float32),
            pltpu.VMEM((2 * row_total, width), jnp.bfloat16),
        ],
        name="paganin",
    )(forward, back, factors, intensity)


def send_scale(largest, angle_total, voxel_edge):
    limit = send_bound / (angle_total * voxel_edge * thickness_bound)
    scale = jnp.float32(1.0)
    for bits in (32, 16, 8, 4, 2, 1):
        wider = scale * float(2**bits)
        scale = jnp.where(largest * wider <= limit, wider, scale)
    return scale


def backproject_kernel(
    place_ref, counts_ref, segment_ref, tile_ref, order_ref, tiles_ref, *refs
):
    *thickness_refs, out_ref, unscale_ref, rows_ref = refs
    group_total, block_total, capacity, edge = out_ref.shape
    source_total = len(thickness_refs)
    angle_count, _, row_total, _ = thickness_refs[0].shape
    group, tile = place_ref[0], place_ref[1]
    largest = jnp.max(jnp.abs(tiles_ref[...].astype(jnp.float32)))
    scale = send_scale(largest, angle_count * source_total, edge)
    unscale_ref[...] = jnp.full(unscale_ref.shape, 1.0, jnp.float32) / scale
    starts = [jnp.int32(0)]
    for g in range(group_total - 1):
        starts.append(starts[-1] + counts_ref[g])
    rows_ref[:, row_total:] = jnp.zeros((rows_ref.shape[0], capacity, edge), jnp.float32)

    def one_block(block, slot):
        voxel_block = order_ref[tile * block_total + block]
        pieces, matrices = [], []
        for shift, thickness_ref in enumerate(thickness_refs):
            source = lax.rem(tile + source_total - shift, source_total)
            for local in range(angle_count):
                angle = (group * source_total + source) * angle_count + local
                pieces.append(thickness_ref[local, segment_ref[angle, voxel_block]])
                matrices.append(tiles_ref[tile_ref[angle, voxel_block]])
        total = jnp.dot(
            jnp.concatenate(pieces, axis=1),
            jnp.concatenate(matrices, axis=0),
            preferred_element_type=jnp.float32,
        )
        rows_ref[slot, :row_total] = total * scale
        for g in range(group_total):
            out_ref[g, block] = rows_ref[slot, pl.ds(starts[g], capacity), :]

    depth = rows_ref.shape[0]

    def some_blocks(step, carry):
        for slot in range(depth):
            one_block(step * depth + slot, slot)
        return carry

    lax.fori_loop(0, block_total // depth, some_blocks, 0)


def backproject(place, counts, segment_ids, tile_ids, block_order, tiles, thickness, group_total, capacity):
    source_total = len(thickness)
    row_total, edge = thickness[0].shape[2:]
    block_total = block_order.shape[0] // source_total
    depth = 2 if block_total % 2 == 0 else 1
    scalars = pl.BlockSpec(memory_space=pltpu.SMEM)
    vectors = pl.BlockSpec(memory_space=pltpu.VMEM)
    return pl.pallas_call(
        backproject_kernel,
        in_specs=[scalars] * 5 + [vectors] * (1 + source_total),
        out_specs=[vectors, vectors],
        out_shape=[
            jax.ShapeDtypeStruct((group_total, block_total, capacity, edge), jnp.float32),
            jax.ShapeDtypeStruct((8, edge), jnp.float32),
        ],
        scratch_shapes=[pltpu.VMEM((depth, row_total + capacity, edge), jnp.float32)],
        name="backproject",
    )(place, counts, segment_ids, tile_ids, block_order, tiles, *thickness)


def per_device(intensity, counts, segment_ids, tile_ids, block_order, tiles):
    row_total = intensity.shape[1]
    voxel_edge = tiles.shape[1]
    group_total = lax.axis_size("angle")
    tile_total = lax.axis_size("tile")
    capacity = 2 * row_total // group_total
    thickness = paganin_thickness(intensity, voxel_edge)
    sources = [thickness]
    for shift in range(1, tile_total):
        ring = [(i, (i + shift) % tile_total) for i in range(tile_total)]
        sources.append(lax.ppermute(thickness, "tile", ring))
    place = jnp.stack([lax.axis_index("angle"), lax.axis_index("tile")]).astype(jnp.int32)
    partial, unscale = backproject(
        place, counts, segment_ids, tile_ids, block_order, tiles, sources, group_total, capacity
    )
    arrived = lax.all_to_all(partial.astype(jnp.float16), "angle", split_axis=0, concat_axis=0, tiled=True)
    volume = jnp.sum(arrived.astype(jnp.float32), axis=0) * unscale[0, 0]
    slot_valid = jnp.arange(capacity, dtype=jnp.int32) < counts[lax.axis_index("angle")]
    volume = jnp.where(slot_valid[None, :, None], volume, 0.0)
    return jnp.swapaxes(volume, 0, 1)[None]


def solution(mesh):
    in_specs = (P(("groups", "angle", "tile"), None, None), P("groups"), P(), P(), P("groups"), P())
    out_specs = P(("groups", "angle"), None, "tile", None)
    return jax.shard_map(
        per_device, mesh=mesh, in_specs=in_specs, out_specs=out_specs, check_vma=False
    )
```

```python
import functools
import math

import jax
import jax.numpy as jnp
import numpy as np
from jax import lax
from jax.experimental import pallas as pl
from jax.experimental.pallas import tpu as pltpu
from jax.sharding import PartitionSpec as P

paganin_alpha = 2.0
lanes = 128
sublanes = 8
strands = 8
chunks = strands * sublanes
pitch_pad = 8
thickness_bound = 1.75
send_bound = 60000.0


def split_parts(values):
    high = values.astype(jnp.bfloat16)
    low = (values - high.astype(jnp.float32)).astype(jnp.bfloat16)
    return high, low


def paired_parts(values):
    high, low = split_parts(values)
    return jnp.concatenate([high, low, high], axis=1)


def paired_table(matrix, axis):
    high = matrix.astype(jnp.bfloat16)
    low = (matrix - high.astype(np.float64)).astype(jnp.bfloat16)
    return jnp.asarray(np.concatenate([high, high, low], axis=axis))


def filter_tables(row_total, chunk):
    index = np.arange(row_total)
    phase = 2.0 * np.pi / row_total * (index[:, None] * index[None, :] % row_total)
    hartley = (np.cos(phase) + np.sin(phase)) / math.sqrt(row_total)
    row_weight = 4.0 * np.square(np.sin(np.pi * index / row_total))
    half = (1.0 + paganin_alpha * (row_weight + 2.0)) / (2.0 * paganin_alpha)
    root = half - np.sqrt(half * half - 1.0)
    levels = chunks.bit_length() - 1
    powers = [root] + [root ** (chunk << s) for s in range(levels)]
    powers.append(1.0 / (1.0 - root ** (chunk * chunks)))
    powers = np.repeat(np.stack(powers), sublanes, axis=0).astype(np.float32)
    back = hartley * (root / paganin_alpha)[None, :]
    return paired_table(hartley, 0), paired_table(back, 1), jnp.asarray(powers)


def chunk_shift(values, distance):
    moved = []
    for q in range(strands):
        turns, source = divmod(q - distance, strands)
        moved.append(pltpu.roll(values[source], -turns % sublanes, 0) if turns % sublanes else values[source])
    return moved


def carries(ends, powers_ref, direction):
    levels = chunks.bit_length() - 1
    for s in range(levels):
        power = powers_ref[pl.ds((1 + s) * sublanes, sublanes), :]
        before = chunk_shift(ends, direction << s)
        ends = [end + power * other for end, other in zip(ends, before)]
    whole = powers_ref[pl.ds((1 + levels) * sublanes, sublanes), :]
    return [whole * other for other in chunk_shift(ends, direction)]


def filter_kernel(forward_ref, back_ref, powers_ref, f_ref, out_ref, modes_ref):
    row_total, width = f_ref.shape[1:]
    edge = out_ref.shape[3]
    span = width // sublanes
    pitch = modes_ref.shape[0] // sublanes
    chunk = span // strands

    def place(column):
        return column // span * pitch + column % span

    for column in range(0, width, lanes):
        turned = f_ref[0, :, column : column + lanes].T
        modes_ref[pl.ds(place(column), lanes), :] = jnp.dot(
            paired_parts(turned), forward_ref[...], preferred_element_type=jnp.float32
        )

    root = powers_ref[pl.ds(0, sublanes), :]

    def strand(q, step):
        return pl.ds(q * chunk + step, sublanes, stride=pitch)

    def sweep(values, order, keep):
        for step in order:
            for q in range(strands):
                values[q] = modes_ref[strand(q, step), :] + root * values[q]
                if keep:
                    modes_ref[strand(q, step), :] = values[q]
        return values

    for direction in (1, -1):
        order = range(chunk)[::direction]
        zeros = [jnp.zeros((sublanes, row_total), jnp.float32)] * strands
        ends = sweep(zeros, order, False)
        sweep(carries(ends, powers_ref, direction), order, True)

    for column in range(0, width, lanes):
        filtered = lax.dot_general(
            back_ref[...],
            paired_parts(modes_ref[pl.ds(place(column), lanes), :]),
            (((1,), (1,)), ((), ())),
            preferred_element_type=jnp.float32,
        )
        thickness = (-jnp.log(filtered)).astype(jnp.bfloat16)
        for part in range(lanes // edge):
            out_ref[0, column // edge + part] = thickness[:, part * edge : (part + 1) * edge]


def paganin_thickness(intensity, voxel_edge):
    angle_count, row_total, width = intensity.shape
    assert row_total == lanes and width % (sublanes * lanes) == 0 and lanes % voxel_edge == 0
    forward, back, powers = filter_tables(row_total, width // chunks)
    segments = width // voxel_edge
    whole = lambda a: (0, 0)
    return pl.pallas_call(
        filter_kernel,
        grid=(angle_count,),
        in_specs=[
            pl.BlockSpec(forward.shape, whole),
            pl.BlockSpec(back.shape, whole),
            pl.BlockSpec(powers.shape, whole),
            pl.BlockSpec((1, row_total, width), lambda a: (a, 0, 0)),
        ],
        out_specs=pl.BlockSpec((1, segments, row_total, voxel_edge), lambda a: (a, 0, 0, 0)),
        out_shape=jax.ShapeDtypeStruct((angle_count, segments, row_total, voxel_edge), jnp.bfloat16),
        scratch_shapes=[pltpu.VMEM((width + sublanes * pitch_pad, row_total), jnp.float32)],
        name="paganin",
    )(forward, back, powers, intensity)


def send_scale(largest, angle_total, voxel_edge):
    limit = send_bound / (angle_total * voxel_edge * thickness_bound)
    scale = jnp.float32(1.0)
    for bits in (32, 16, 8, 4, 2, 1):
        wider = scale * float(2**bits)
        scale = jnp.where(largest * wider <= limit, wider, scale)
    return scale


def backproject_kernel(
    place_ref, counts_ref, segment_ref, tile_ref, order_ref, tiles_ref, *refs
):
    *thickness_refs, out_ref, unscale_ref, rows_ref = refs
    group_total, block_total, capacity, edge = out_ref.shape
    source_total = len(thickness_refs)
    angle_count, _, row_total, _ = thickness_refs[0].shape
    group, tile = place_ref[0], place_ref[1]
    largest = jnp.max(jnp.abs(tiles_ref[...].astype(jnp.float32)))
    scale = send_scale(largest, angle_count * source_total, edge)
    unscale_ref[...] = jnp.full(unscale_ref.shape, 1.0, jnp.float32) / scale
    starts = [jnp.int32(0)]
    for g in range(group_total - 1):
        starts.append(starts[-1] + counts_ref[g])
    rows_ref[:, row_total:] = jnp.zeros((rows_ref.shape[0], capacity, edge), jnp.float32)

    def one_block(block, slot):
        voxel_block = order_ref[tile * block_total + block]
        pieces, matrices = [], []
        for shift, thickness_ref in enumerate(thickness_refs):
            source = lax.rem(tile + source_total - shift, source_total)
            for local in range(angle_count):
                angle = (group * source_total + source) * angle_count + local
                pieces.append(thickness_ref[local, segment_ref[angle, voxel_block]])
                matrices.append(tiles_ref[tile_ref[angle, voxel_block]])
        total = jnp.dot(
            jnp.concatenate(pieces, axis=1),
            jnp.concatenate(matrices, axis=0),
            preferred_element_type=jnp.float32,
        )
        rows_ref[slot, :row_total] = total * scale
        for g in range(group_total):
            out_ref[g, block] = rows_ref[slot, pl.ds(starts[g], capacity), :]

    depth = rows_ref.shape[0]

    def some_blocks(step, carry):
        for slot in range(depth):
            one_block(step * depth + slot, slot)
        return carry

    lax.fori_loop(0, block_total // depth, some_blocks, 0)


def backproject(place, counts, segment_ids, tile_ids, block_order, tiles, thickness, group_total, capacity):
    source_total = len(thickness)
    row_total, edge = thickness[0].shape[2:]
    block_total = block_order.shape[0] // source_total
    depth = 2 if block_total % 2 == 0 else 1
    scalars = pl.BlockSpec(memory_space=pltpu.SMEM)
    vectors = pl.BlockSpec(memory_space=pltpu.VMEM)
    return pl.pallas_call(
        backproject_kernel,
        in_specs=[scalars] * 5 + [vectors] * (1 + source_total),
        out_specs=[vectors, vectors],
        out_shape=[
            jax.ShapeDtypeStruct((group_total, block_total, capacity, edge), jnp.float32),
            jax.ShapeDtypeStruct((8, edge), jnp.float32),
        ],
        scratch_shapes=[pltpu.VMEM((depth, row_total + capacity, edge), jnp.float32)],
        name="backproject",
    )(place, counts, segment_ids, tile_ids, block_order, tiles, *thickness)


def per_device(intensity, counts, segment_ids, tile_ids, block_order, tiles):
    row_total = intensity.shape[1]
    voxel_edge = tiles.shape[1]
    group_total = lax.axis_size("angle")
    tile_total = lax.axis_size("tile")
    capacity = 2 * row_total // group_total
    thickness = paganin_thickness(intensity, voxel_edge)
    sources = [thickness]
    for shift in range(1, tile_total):
        ring = [(i, (i + shift) % tile_total) for i in range(tile_total)]
        sources.append(lax.ppermute(thickness, "tile", ring))
    place = jnp.stack([lax.axis_index("angle"), lax.axis_index("tile")]).astype(jnp.int32)
    partial, unscale = backproject(
        place, counts, segment_ids, tile_ids, block_order, tiles, sources, group_total, capacity
    )
    arrived = lax.all_to_all(partial.astype(jnp.float16), "angle", split_axis=0, concat_axis=0, tiled=True)
    volume = jnp.sum(arrived.astype(jnp.float32), axis=0) * unscale[0, 0]
    slot_valid = jnp.arange(capacity, dtype=jnp.int32) < counts[lax.axis_index("angle")]
    volume = jnp.where(slot_valid[None, :, None], volume, 0.0)
    return jnp.swapaxes(volume, 0, 1)[None]


def solution(mesh):
    in_specs = (P(("groups", "angle", "tile"), None, None), P("groups"), P(), P(), P("groups"), P())
    out_specs = P(("groups", "angle"), None, "tile", None)
    return jax.shard_map(
        per_device, mesh=mesh, in_specs=in_specs, out_specs=out_specs, check_vma=False
    )
```

```python
import functools
import math

import jax
import jax.numpy as jnp
import numpy as np
from jax import lax
from jax.experimental import pallas as pl
from jax.experimental.pallas import tpu as pltpu
from jax.sharding import PartitionSpec as P

paganin_alpha = 2.0
lanes = 128
sublanes = 8
strands = 8
chunks = strands * sublanes
pitch_pad = 8
thickness_bound = 1.75
send_bound = 60000.0


def split_parts(values):
    high = values.astype(jnp.bfloat16)
    low = (values - high.astype(jnp.float32)).astype(jnp.bfloat16)
    return high, low


def paired_parts(values):
    high, low = split_parts(values)
    return jnp.concatenate([high, low, high], axis=1)


def paired_table(matrix, axis):
    high = matrix.astype(jnp.bfloat16)
    low = (matrix - high.astype(np.float64)).astype(jnp.bfloat16)
    return jnp.asarray(np.concatenate([high, high, low], axis=axis))


def filter_tables(row_total, chunk):
    index = np.arange(row_total)
    phase = 2.0 * np.pi / row_total * (index[:, None] * index[None, :] % row_total)
    hartley = (np.cos(phase) + np.sin(phase)) / math.sqrt(row_total)
    row_weight = 4.0 * np.square(np.sin(np.pi * index / row_total))
    half = (1.0 + paganin_alpha * (row_weight + 2.0)) / (2.0 * paganin_alpha)
    root = half - np.sqrt(half * half - 1.0)
    levels = chunks.bit_length() - 1
    powers = [root] + [root ** (chunk << s) for s in range(levels)]
    powers.append(1.0 / (1.0 - root ** (chunk * chunks)))
    powers = np.repeat(np.stack(powers), sublanes, axis=0).astype(np.float32)
    back = hartley * (root / paganin_alpha)[None, :]
    return paired_table(hartley, 0), paired_table(back, 1), jnp.asarray(powers)


def chunk_shift(values, distance):
    moved = []
    for q in range(strands):
        turns, source = divmod(q - distance, strands)
        moved.append(pltpu.roll(values[source], -turns % sublanes, 0) if turns % sublanes else values[source])
    return moved


def carries(ends, powers_ref, direction):
    levels = chunks.bit_length() - 1
    for s in range(levels):
        power = powers_ref[pl.ds((1 + s) * sublanes, sublanes), :]
        before = chunk_shift(ends, direction << s)
        ends = [end + power * other for end, other in zip(ends, before)]
    whole = powers_ref[pl.ds((1 + levels) * sublanes, sublanes), :]
    return [whole * other for other in chunk_shift(ends, direction)]


def filter_kernel(forward_ref, back_ref, powers_ref, f_ref, out_ref, modes_ref):
    row_total, width = f_ref.shape[1:]
    edge = out_ref.shape[3]
    span = width // sublanes
    pitch = modes_ref.shape[0] // sublanes
    chunk = span // strands

    def place(column):
        return column // span * pitch + column % span

    for column in range(0, width, lanes):
        turned = f_ref[0, :, column : column + lanes].T
        modes_ref[pl.ds(place(column), lanes), :] = jnp.dot(
            paired_parts(turned), forward_ref[...], preferred_element_type=jnp.float32
        )

    root = powers_ref[pl.ds(0, sublanes), :]

    def strand(q, step):
        return pl.ds(q * chunk + step, sublanes, stride=pitch)

    def sweep(values, order, keep):
        for step in order:
            for q in range(strands):
                values[q] = modes_ref[strand(q, step), :] + root * values[q]
                if keep:
                    modes_ref[strand(q, step), :] = values[q]
        return values

    for direction in (1, -1):
        order = range(chunk)[::direction]
        zeros = [jnp.zeros((sublanes, row_total), jnp.float32)] * strands
        ends = sweep(zeros, order, False)
        sweep(carries(ends, powers_ref, direction), order, True)

    for column in range(0, width, lanes):
        filtered = lax.dot_general(
            back_ref[...],
            paired_parts(modes_ref[pl.ds(place(column), lanes), :]),
            (((1,), (1,)), ((), ())),
            preferred_element_type=jnp.float32,
        )
        thickness = (-jnp.log(filtered)).astype(jnp.bfloat16)
        for part in range(lanes // edge):
            out_ref[0, column // edge + part] = thickness[:, part * edge : (part + 1) * edge]


def paganin_thickness(intensity, voxel_edge):
    angle_count, row_total, width = intensity.shape
    assert row_total == lanes and width % (sublanes * lanes) == 0 and lanes % voxel_edge == 0
    forward, back, powers = filter_tables(row_total, width // chunks)
    segments = width // voxel_edge
    whole = lambda a: (0, 0)
    return pl.pallas_call(
        filter_kernel,
        grid=(angle_count,),
        in_specs=[
            pl.BlockSpec(forward.shape, whole),
            pl.BlockSpec(back.shape, whole),
            pl.BlockSpec(powers.shape, whole),
            pl.BlockSpec((1, row_total, width), lambda a: (a, 0, 0)),
        ],
        out_specs=pl.BlockSpec((1, segments, row_total, voxel_edge), lambda a: (a, 0, 0, 0)),
        out_shape=jax.ShapeDtypeStruct((angle_count, segments, row_total, voxel_edge), jnp.bfloat16),
        scratch_shapes=[pltpu.VMEM((width + sublanes * pitch_pad, row_total), jnp.float32)],
        name="paganin",
    )(forward, back, powers, intensity)


def send_scale(largest, angle_total, voxel_edge):
    limit = send_bound / (angle_total * voxel_edge * thickness_bound)
    scale = jnp.float32(1.0)
    for bits in (32, 16, 8, 4, 2, 1):
        wider = scale * float(2**bits)
        scale = jnp.where(largest * wider <= limit, wider, scale)
    return scale


def backproject_kernel(
    partners, place_ref, segment_ref, tile_ref, order_ref, tiles_ref, *refs
):
    *thickness_refs, out_ref, unscale_ref = refs
    chunk_total, share, row_total, edge = out_ref.shape
    source_total = len(thickness_refs)
    angle_count = thickness_refs[0].shape[0]
    group, tile, group_total = place_ref[0], place_ref[1], place_ref[2]
    largest = jnp.max(jnp.abs(tiles_ref[...].astype(jnp.float32)))
    scale = send_scale(largest, angle_count * source_total, edge)
    unscale_ref[...] = jnp.full(unscale_ref.shape, 1.0, jnp.float32) / scale

    for chunk, partner in enumerate(partners):
        owner = lax.bitwise_xor(group, jnp.int32(partner))
        for block in range(share):
            voxel_block = order_ref[(tile * group_total + owner) * share + block]
            pieces, matrices = [], []
            for shift, thickness_ref in enumerate(thickness_refs):
                source = lax.rem(tile + source_total - shift, source_total)
                for local in range(angle_count):
                    angle = (group * source_total + source) * angle_count + local
                    pieces.append(thickness_ref[local, segment_ref[angle, voxel_block]])
                    matrices.append(tiles_ref[tile_ref[angle, voxel_block]])
            total = jnp.dot(
                jnp.concatenate(pieces, axis=1),
                jnp.concatenate(matrices, axis=0),
                preferred_element_type=jnp.float32,
            )
            out_ref[chunk, block] = total * scale


def backproject(partners, place, segment_ids, tile_ids, block_order, tiles, thickness, share):
    row_total, edge = thickness[0].shape[2:]
    angle_total = thickness[0].shape[0] * len(thickness)
    blocks = len(partners) * share
    scalars = pl.BlockSpec(memory_space=pltpu.SMEM)
    vectors = pl.BlockSpec(memory_space=pltpu.VMEM)
    return pl.pallas_call(
        functools.partial(backproject_kernel, tuple(partners)),
        in_specs=[scalars] * 4 + [vectors] * (1 + len(thickness)),
        out_specs=[vectors, vectors],
        out_shape=[
            jax.ShapeDtypeStruct((len(partners), share, row_total, edge), jnp.float32),
            jax.ShapeDtypeStruct((8, edge), jnp.float32),
        ],
        cost_estimate=pl.CostEstimate(
            flops=2 * blocks * angle_total * row_total * edge * edge,
            bytes_accessed=4 * blocks * row_total * edge,
            transcendentals=0,
        ),
        name="backproject",
    )(place, segment_ids, tile_ids, block_order, tiles, *thickness)


def regroup_kernel(counts_ref, rows_ref, out_ref, padded_ref):
    group_total, share, capacity, edge = out_ref.shape
    row_total = rows_ref.shape[1]
    for block in range(share):
        padded_ref[block, :row_total] = rows_ref[block]
        padded_ref[block, row_total:] = jnp.zeros((capacity, edge), jnp.float32)
    start = 0
    for g in range(group_total):
        for block in range(share):
            out_ref[g, block] = padded_ref[block, pl.ds(start, capacity), :]
        start = start + counts_ref[g]


def regroup(counts, rows, group_total, capacity):
    share, row_total, edge = rows.shape
    return pl.pallas_call(
        regroup_kernel,
        in_specs=[pl.BlockSpec(memory_space=pltpu.SMEM), pl.BlockSpec(memory_space=pltpu.VMEM)],
        out_specs=pl.BlockSpec(memory_space=pltpu.VMEM),
        out_shape=jax.ShapeDtypeStruct((group_total, share, capacity, edge), jnp.float32),
        scratch_shapes=[pltpu.VMEM((share, row_total + capacity, edge), jnp.float32)],
        name="regroup",
    )(counts, rows)


def per_device(intensity, counts, segment_ids, tile_ids, block_order, tiles):
    row_total = intensity.shape[1]
    voxel_edge = tiles.shape[1]
    group_total = lax.axis_size("angle")
    tile_total = lax.axis_size("tile")
    group = lax.axis_index("angle")
    capacity = 2 * row_total // group_total
    share = block_order.shape[0] // (tile_total * group_total)
    assert group_total & (group_total - 1) == 0
    thickness = paganin_thickness(intensity, voxel_edge)
    sources = [thickness]
    for shift in range(1, tile_total):
        ring = [(i, (i + shift) % tile_total) for i in range(tile_total)]
        sources.append(lax.ppermute(thickness, "tile", ring))
    place = jnp.stack([group, lax.axis_index("tile"), jnp.int32(group_total)]).astype(jnp.int32)
    tables = (place, segment_ids, tile_ids, block_order, tiles, sources, share)
    half = max(1, group_total // 2)
    far, unscale = backproject(range(half, group_total)[::-1], *tables)
    parts = []
    for partner, partial in zip(range(half, group_total)[::-1], far):
        swap = [(i, i ^ partner) for i in range(group_total)]
        parts.append(lax.ppermute(partial.astype(jnp.float16), "angle", swap))
    near, _ = backproject(range(half)[::-1], *tables)
    for partner, partial in zip(range(half)[::-1], near):
        swap = [(i, i ^ partner) for i in range(group_total)]
        if partner:
            parts.append(lax.ppermute(partial.astype(jnp.float16), "angle", swap))
    rows = near[half - 1]
    for part in parts:
        rows = rows + part.astype(jnp.float32)
    slots = regroup(counts, rows, group_total, capacity) * (1.0 / group_total)
    arrived = lax.all_to_all(slots.astype(jnp.float16), "angle", split_axis=0, concat_axis=0, tiled=True)
    arrived = arrived.reshape(group_total * share, capacity, voxel_edge)
    volume = arrived.astype(jnp.float32) * (unscale[0, 0] * group_total)
    slot_valid = jnp.arange(capacity, dtype=jnp.int32) < counts[group]
    volume = jnp.where(slot_valid[None, :, None], volume, 0.0)
    return jnp.swapaxes(volume, 0, 1)[None]


def solution(mesh):
    in_specs = (P(("groups", "angle", "tile"), None, None), P("groups"), P(), P(), P("groups"), P())
    out_specs = P(("groups", "angle"), None, "tile", None)
    return jax.shard_map(
        per_device, mesh=mesh, in_specs=in_specs, out_specs=out_specs, check_vma=False
    )
```

```python
import functools
import math

import jax
import jax.numpy as jnp
import numpy as np
from jax import lax
from jax.experimental import pallas as pl
from jax.experimental.pallas import tpu as pltpu
from jax.sharding import PartitionSpec as P

paganin_alpha = 2.0
lanes = 128
sublanes = 8
strands = 16
chunks = strands * sublanes
pitch_pad = 8
kernel_vmem = 24 << 20
thickness_bound = 1.75
send_bound = 60000.0


def split_parts(values):
    high = values.astype(jnp.bfloat16)
    low = (values - high.astype(jnp.float32)).astype(jnp.bfloat16)
    return high, low


def paired_parts(values):
    high, low = split_parts(values)
    return jnp.concatenate([high, low, high], axis=1)


def paired_table(matrix, axis):
    high = matrix.astype(jnp.bfloat16)
    low = (matrix - high.astype(np.float64)).astype(jnp.bfloat16)
    return jnp.asarray(np.concatenate([high, high, low], axis=axis))


def filter_tables(row_total, chunk):
    index = np.arange(row_total)
    phase = 2.0 * np.pi / row_total * (index[:, None] * index[None, :] % row_total)
    hartley = (np.cos(phase) + np.sin(phase)) / math.sqrt(row_total)
    row_weight = 4.0 * np.square(np.sin(np.pi * index / row_total))
    half = (1.0 + paganin_alpha * (row_weight + 2.0)) / (2.0 * paganin_alpha)
    root = half - np.sqrt(half * half - 1.0)
    levels = chunks.bit_length() - 1
    powers = [root] + [root ** (chunk << s) for s in range(levels)]
    powers.append(1.0 / (1.0 - root ** (chunk * chunks)))
    powers = np.repeat(np.stack(powers), sublanes, axis=0).astype(np.float32)
    back = hartley * (root / paganin_alpha)[None, :]
    return paired_table(hartley, 0), paired_table(back, 1), jnp.asarray(powers)


def chunk_shift(values, distance):
    moved = []
    for q in range(strands):
        turns, source = divmod(q - distance, strands)
        moved.append(pltpu.roll(values[source], -turns % sublanes, 0) if turns % sublanes else values[source])
    return moved


def carries(ends, powers_ref, direction):
    levels = chunks.bit_length() - 1
    for s in range(levels):
        power = powers_ref[pl.ds((1 + s) * sublanes, sublanes), :]
        before = chunk_shift(ends, direction << s)
        ends = [end + power * other for end, other in zip(ends, before)]
    whole = powers_ref[pl.ds((1 + levels) * sublanes, sublanes), :]
    return [whole * other for other in chunk_shift(ends, direction)]


def filter_kernel(forward_ref, back_ref, powers_ref, f_ref, out_ref, modes_ref):
    row_total, width = f_ref.shape[1:]
    edge = out_ref.shape[3]
    span = width // sublanes
    pitch = modes_ref.shape[0] // sublanes
    chunk = span // strands

    def place(column):
        return column // span * pitch + column % span

    for column in range(0, width, span):
        turned = [f_ref[0, :, start : start + lanes].T for start in range(column, column + span, lanes)]
        modes_ref[pl.ds(place(column), span), :] = jnp.dot(
            paired_parts(jnp.concatenate(turned, axis=0)), forward_ref[...], preferred_element_type=jnp.float32
        )

    root = powers_ref[pl.ds(0, sublanes), :]

    def strand(q, step):
        return pl.ds(q * chunk + step, sublanes, stride=pitch)

    def sweep(values, order, keep):
        for step in order:
            for q in range(strands):
                values[q] = modes_ref[strand(q, step), :] + root * values[q]
                if keep:
                    modes_ref[strand(q, step), :] = values[q]
        return values

    for direction in (1, -1):
        order = range(chunk)[::direction]
        zeros = [jnp.zeros((sublanes, row_total), jnp.float32)] * strands
        ends = sweep(zeros, order, False)
        sweep(carries(ends, powers_ref, direction), order, True)

    for column in range(0, width, span):
        filtered = lax.dot_general(
            back_ref[...],
            paired_parts(modes_ref[pl.ds(place(column), span), :]),
            (((1,), (1,)), ((), ())),
            preferred_element_type=jnp.float32,
        )
        thickness = (-jnp.log(filtered)).astype(jnp.bfloat16)
        for part in range(span // edge):
            out_ref[0, column // edge + part] = thickness[:, part * edge : (part + 1) * edge]


def paganin_thickness(intensity, voxel_edge):
    angle_count, row_total, width = intensity.shape
    assert row_total == lanes and width % (sublanes * lanes) == 0 and lanes % voxel_edge == 0
    forward, back, powers = filter_tables(row_total, width // chunks)
    segments = width // voxel_edge
    whole = lambda a: (0, 0)
    return pl.pallas_call(
        filter_kernel,
        grid=(angle_count,),
        in_specs=[
            pl.BlockSpec(forward.shape, whole),
            pl.BlockSpec(back.shape, whole),
            pl.BlockSpec(powers.shape, whole),
            pl.BlockSpec((1, row_total, width), lambda a: (a, 0, 0)),
        ],
        out_specs=pl.BlockSpec((1, segments, row_total, voxel_edge), lambda a: (a, 0, 0, 0)),
        out_shape=jax.ShapeDtypeStruct((angle_count, segments, row_total, voxel_edge), jnp.bfloat16),
        scratch_shapes=[pltpu.VMEM((width + sublanes * pitch_pad, row_total), jnp.float32)],
        compiler_params=pltpu.CompilerParams(vmem_limit_bytes=kernel_vmem),
        name="paganin",
    )(*[pltpu.with_memory_space_constraint(v, pltpu.HBM) for v in (forward, back, powers, intensity)])


def send_scale(largest, angle_total, voxel_edge):
    limit = send_bound / (angle_total * voxel_edge * thickness_bound)
    scale = jnp.float32(1.0)
    for bits in (32, 16, 8, 4, 2, 1):
        wider = scale * float(2**bits)
        scale = jnp.where(largest * wider <= limit, wider, scale)
    return scale


def backproject_kernel(
    partners, place_ref, segment_ref, tile_ref, order_ref, tiles_ref, *refs
):
    *thickness_refs, out_ref, unscale_ref = refs
    chunk_total, share, row_total, edge = out_ref.shape
    source_total = len(thickness_refs)
    angle_count = thickness_refs[0].shape[0]
    group, tile, group_total = place_ref[0], place_ref[1], place_ref[2]
    largest = jnp.max(jnp.abs(tiles_ref[...].astype(jnp.float32)))
    scale = send_scale(largest, angle_count * source_total, edge)
    unscale_ref[...] = jnp.full(unscale_ref.shape, 1.0, jnp.float32) / scale

    for chunk, partner in enumerate(partners):
        owner = lax.bitwise_xor(group, jnp.int32(partner))
        for block in range(share):
            voxel_block = order_ref[(tile * group_total + owner) * share + block]
            pieces, matrices = [], []
            for shift, thickness_ref in enumerate(thickness_refs):
                source = lax.rem(tile + source_total - shift, source_total)
                for local in range(angle_count):
                    angle = (group * source_total + source) * angle_count + local
                    pieces.append(thickness_ref[local, segment_ref[angle, voxel_block]])
                    matrices.append(tiles_ref[tile_ref[angle, voxel_block]])
            total = jnp.dot(
                jnp.concatenate(pieces, axis=1),
                jnp.concatenate(matrices, axis=0),
                preferred_element_type=jnp.float32,
            )
            out_ref[chunk, block] = total * scale


def resident(values):
    return pltpu.with_memory_space_constraint(values, pltpu.VMEM)


def backproject(partners, place, segment_ids, tile_ids, block_order, tiles, thickness, share):
    row_total, edge = thickness[0].shape[2:]
    angle_total = thickness[0].shape[0] * len(thickness)
    blocks = len(partners) * share
    scalars = pl.BlockSpec(memory_space=pltpu.SMEM)
    vectors = pl.BlockSpec(memory_space=pltpu.VMEM)
    return pl.pallas_call(
        functools.partial(backproject_kernel, tuple(partners)),
        in_specs=[scalars] * 4 + [vectors] * (1 + len(thickness)),
        out_specs=[vectors, vectors],
        out_shape=[
            jax.ShapeDtypeStruct((len(partners), share, row_total, edge), jnp.float32),
            jax.ShapeDtypeStruct((8, edge), jnp.float32),
        ],
        cost_estimate=pl.CostEstimate(
            flops=2 * blocks * angle_total * row_total * edge * edge,
            bytes_accessed=4 * blocks * row_total * edge,
            transcendentals=0,
        ),
        compiler_params=pltpu.CompilerParams(vmem_limit_bytes=kernel_vmem),
        name="backproject",
    )(place, segment_ids, tile_ids, block_order, tiles, *[resident(t) for t in thickness])


def regroup_kernel(counts_ref, rows_ref, out_ref, padded_ref):
    group_total, share, capacity, edge = out_ref.shape
    row_total = rows_ref.shape[1]
    for block in range(share):
        padded_ref[block, :row_total] = rows_ref[block]
        padded_ref[block, row_total:] = jnp.zeros((capacity, edge), jnp.float32)
    start = 0
    for g in range(group_total):
        for block in range(share):
            out_ref[g, block] = padded_ref[block, pl.ds(start, capacity), :]
        start = start + counts_ref[g]


def regroup(counts, rows, group_total, capacity):
    share, row_total, edge = rows.shape
    return pl.pallas_call(
        regroup_kernel,
        in_specs=[pl.BlockSpec(memory_space=pltpu.SMEM), pl.BlockSpec(memory_space=pltpu.VMEM)],
        out_specs=pl.BlockSpec(memory_space=pltpu.VMEM),
        out_shape=jax.ShapeDtypeStruct((group_total, share, capacity, edge), jnp.float32),
        scratch_shapes=[pltpu.VMEM((share, row_total + capacity, edge), jnp.float32)],
        compiler_params=pltpu.CompilerParams(vmem_limit_bytes=kernel_vmem),
        name="regroup",
    )(counts, rows)


def per_device(intensity, counts, segment_ids, tile_ids, block_order, tiles):
    row_total = intensity.shape[1]
    voxel_edge = tiles.shape[1]
    group_total = lax.axis_size("angle")
    tile_total = lax.axis_size("tile")
    group = lax.axis_index("angle")
    capacity = 2 * row_total // group_total
    share = block_order.shape[0] // (tile_total * group_total)
    assert group_total & (group_total - 1) == 0
    thickness = paganin_thickness(intensity, voxel_edge)
    sources = [thickness]
    for shift in range(1, tile_total):
        ring = [(i, (i + shift) % tile_total) for i in range(tile_total)]
        sources.append(lax.ppermute(thickness, "tile", ring))
    place = jnp.stack([group, lax.axis_index("tile"), jnp.int32(group_total)]).astype(jnp.int32)
    tables = (place, segment_ids, tile_ids, block_order, tiles, sources, share)
    half = max(1, group_total // 2)
    far, unscale = backproject(range(half, group_total)[::-1], *tables)
    parts = []
    for partner, partial in zip(range(half, group_total)[::-1], far):
        swap = [(i, i ^ partner) for i in range(group_total)]
        parts.append(lax.ppermute(partial.astype(jnp.float16), "angle", swap))
    near, _ = backproject(range(half)[::-1], *tables)
    for partner, partial in zip(range(half)[::-1], near):
        swap = [(i, i ^ partner) for i in range(group_total)]
        if partner:
            parts.append(lax.ppermute(partial.astype(jnp.float16), "angle", swap))
    rows = near[half - 1]
    for part in parts:
        rows = rows + part.astype(jnp.float32)
    slots = regroup(counts, rows, group_total, capacity) * (1.0 / group_total)
    arrived = lax.all_to_all(slots.astype(jnp.float16), "angle", split_axis=0, concat_axis=0, tiled=True)
    arrived = arrived.reshape(group_total * share, capacity, voxel_edge)
    volume = arrived.astype(jnp.float32) * (unscale[0, 0] * group_total)
    slot_valid = jnp.arange(capacity, dtype=jnp.int32) < counts[group]
    volume = jnp.where(slot_valid[None, :, None], volume, 0.0)
    return jnp.swapaxes(volume, 0, 1)[None]


def solution(mesh):
    in_specs = (P(("groups", "angle", "tile"), None, None), P("groups"), P(), P(), P("groups"), P())
    out_specs = P(("groups", "angle"), None, "tile", None)
    return jax.shard_map(
        per_device, mesh=mesh, in_specs=in_specs, out_specs=out_specs, check_vma=False
    )
```

```python
import functools
import math

import jax
import jax.numpy as jnp
import numpy as np
from jax import lax
from jax.experimental import pallas as pl
from jax.experimental.pallas import tpu as pltpu
from jax.sharding import PartitionSpec as P

paganin_alpha = 2.0
lanes = 128
sublanes = 8
strands = 16
chunks = strands * sublanes
pitch_pad = 8
kernel_vmem = 24 << 20
thickness_bound = 1.75
send_bound = 60000.0


def split_parts(values):
    high = values.astype(jnp.bfloat16)
    low = (values - high.astype(jnp.float32)).astype(jnp.bfloat16)
    return high, low


def paired_parts(values):
    high, low = split_parts(values)
    return jnp.concatenate([high, low, high], axis=1)


def paired_table(matrix, axis):
    high = matrix.astype(jnp.bfloat16)
    low = (matrix - high.astype(np.float64)).astype(jnp.bfloat16)
    return jnp.asarray(np.concatenate([high, high, low], axis=axis))


def filter_tables(row_total, chunk):
    index = np.arange(row_total)
    phase = 2.0 * np.pi / row_total * (index[:, None] * index[None, :] % row_total)
    hartley = (np.cos(phase) + np.sin(phase)) / math.sqrt(row_total)
    row_weight = 4.0 * np.square(np.sin(np.pi * index / row_total))
    half = (1.0 + paganin_alpha * (row_weight + 2.0)) / (2.0 * paganin_alpha)
    root = half - np.sqrt(half * half - 1.0)
    levels = chunks.bit_length() - 1
    powers = [root] + [root ** (chunk << s) for s in range(levels)]
    powers.append(1.0 / (1.0 - root ** (chunk * chunks)))
    powers = np.repeat(np.stack(powers), sublanes, axis=0).astype(np.float32)
    back = hartley * (root / paganin_alpha)[None, :]
    return paired_table(hartley, 0), paired_table(back, 1), jnp.asarray(powers)


def chunk_shift(values, distance):
    moved = []
    for q in range(strands):
        turns, source = divmod(q - distance, strands)
        moved.append(pltpu.roll(values[source], -turns % sublanes, 0) if turns % sublanes else values[source])
    return moved


def carries(ends, powers_ref, direction):
    levels = chunks.bit_length() - 1
    for s in range(levels):
        power = powers_ref[pl.ds((1 + s) * sublanes, sublanes), :]
        before = chunk_shift(ends, direction << s)
        ends = [end + power * other for end, other in zip(ends, before)]
    whole = powers_ref[pl.ds((1 + levels) * sublanes, sublanes), :]
    return [whole * other for other in chunk_shift(ends, direction)]


def filter_kernel(forward_ref, back_ref, powers_ref, f_ref, out_ref, modes_ref):
    row_total, width = f_ref.shape[1:]
    edge = out_ref.shape[3]
    span = width // sublanes
    pitch = modes_ref.shape[0] // sublanes
    chunk = span // strands

    def place(column):
        return column // span * pitch + column % span

    for column in range(0, width, span):
        turned = [f_ref[0, :, start : start + lanes].T for start in range(column, column + span, lanes)]
        modes_ref[pl.ds(place(column), span), :] = jnp.dot(
            paired_parts(jnp.concatenate(turned, axis=0)), forward_ref[...], preferred_element_type=jnp.float32
        )

    root = powers_ref[pl.ds(0, sublanes), :]

    def strand(q, step):
        return pl.ds(q * chunk + step, sublanes, stride=pitch)

    def sweep(values, order, keep):
        for step in order:
            for q in range(strands):
                values[q] = modes_ref[strand(q, step), :] + root * values[q]
                if keep:
                    modes_ref[strand(q, step), :] = values[q]
        return values

    for direction in (1, -1):
        order = range(chunk)[::direction]
        zeros = [jnp.zeros((sublanes, row_total), jnp.float32)] * strands
        ends = sweep(zeros, order, False)
        sweep(carries(ends, powers_ref, direction), order, True)

    for column in range(0, width, span):
        filtered = lax.dot_general(
            back_ref[...],
            paired_parts(modes_ref[pl.ds(place(column), span), :]),
            (((1,), (1,)), ((), ())),
            preferred_element_type=jnp.float32,
        )
        thickness = (-jnp.log(filtered)).astype(jnp.bfloat16)
        for part in range(span // edge):
            out_ref[0, column // edge + part] = thickness[:, part * edge : (part + 1) * edge]


def paganin_thickness(intensity, voxel_edge):
    angle_count, row_total, width = intensity.shape
    assert row_total == lanes and width % (sublanes * lanes) == 0 and lanes % voxel_edge == 0
    forward, back, powers = filter_tables(row_total, width // chunks)
    segments = width // voxel_edge
    whole = lambda a: (0, 0)
    return pl.pallas_call(
        filter_kernel,
        grid=(angle_count,),
        in_specs=[
            pl.BlockSpec(forward.shape, whole),
            pl.BlockSpec(back.shape, whole),
            pl.BlockSpec(powers.shape, whole),
            pl.BlockSpec((1, row_total, width), lambda a: (a, 0, 0)),
        ],
        out_specs=pl.BlockSpec((1, segments, row_total, voxel_edge), lambda a: (a, 0, 0, 0)),
        out_shape=jax.ShapeDtypeStruct((angle_count, segments, row_total, voxel_edge), jnp.bfloat16),
        scratch_shapes=[pltpu.VMEM((width + sublanes * pitch_pad, row_total), jnp.float32)],
        compiler_params=pltpu.CompilerParams(vmem_limit_bytes=kernel_vmem),
        name="paganin",
    )(*[pltpu.with_memory_space_constraint(v, pltpu.HBM) for v in (forward, back, powers, intensity)])


def send_scale(largest, angle_total, voxel_edge):
    limit = send_bound / (angle_total * voxel_edge * thickness_bound)
    scale = jnp.float32(1.0)
    for bits in (32, 16, 8, 4, 2, 1):
        wider = scale * float(2**bits)
        scale = jnp.where(largest * wider <= limit, wider, scale)
    return scale


def backproject_kernel(
    partners, place_ref, segment_ref, tile_ref, order_ref, tiles_ref, *refs
):
    *thickness_refs, out_ref, unscale_ref = refs
    chunk_total, share, row_total, edge = out_ref.shape
    source_total = len(thickness_refs)
    angle_count = thickness_refs[0].shape[0]
    group, tile, group_total = place_ref[0], place_ref[1], place_ref[2]
    largest = jnp.max(jnp.abs(tiles_ref[...].astype(jnp.float32)))
    scale = send_scale(largest, angle_count * source_total, edge)
    unscale_ref[...] = jnp.full(unscale_ref.shape, 1.0, jnp.float32) / scale

    for chunk, partner in enumerate(partners):
        owner = lax.bitwise_xor(group, jnp.int32(partner))
        for block in range(share):
            voxel_block = order_ref[(tile * group_total + owner) * share + block]
            pieces, matrices = [], []
            for shift, thickness_ref in enumerate(thickness_refs):
                source = lax.rem(tile + source_total - shift, source_total)
                for local in range(angle_count):
                    angle = (group * source_total + source) * angle_count + local
                    pieces.append(thickness_ref[local, segment_ref[angle, voxel_block]])
                    matrices.append(tiles_ref[tile_ref[angle, voxel_block]])
            total = jnp.dot(
                jnp.concatenate(pieces, axis=1),
                jnp.concatenate(matrices, axis=0),
                preferred_element_type=jnp.float32,
            )
            out_ref[chunk, block] = total * scale


def resident(values):
    return pltpu.with_memory_space_constraint(values, pltpu.VMEM)


def backproject(partners, place, segment_ids, tile_ids, block_order, tiles, thickness, share):
    row_total, edge = thickness[0].shape[2:]
    angle_total = thickness[0].shape[0] * len(thickness)
    blocks = len(partners) * share
    scalars = pl.BlockSpec(memory_space=pltpu.SMEM)
    vectors = pl.BlockSpec(memory_space=pltpu.VMEM)
    return pl.pallas_call(
        functools.partial(backproject_kernel, tuple(partners)),
        in_specs=[scalars] * 4 + [vectors] * (1 + len(thickness)),
        out_specs=[vectors, vectors],
        out_shape=[
            jax.ShapeDtypeStruct((len(partners), share, row_total, edge), jnp.float32),
            jax.ShapeDtypeStruct((8, edge), jnp.float32),
        ],
        cost_estimate=pl.CostEstimate(
            flops=2 * blocks * angle_total * row_total * edge * edge,
            bytes_accessed=4 * blocks * row_total * edge,
            transcendentals=0,
        ),
        compiler_params=pltpu.CompilerParams(vmem_limit_bytes=kernel_vmem),
        name="backproject",
    )(place, segment_ids, tile_ids, block_order, tiles, *[resident(t) for t in thickness])


def regroup_kernel(counts_ref, rows_ref, out_ref, padded_ref):
    group_total, share, capacity, edge = out_ref.shape
    row_total = rows_ref.shape[1]
    for block in range(share):
        padded_ref[block, :row_total] = rows_ref[block]
        padded_ref[block, row_total:] = jnp.zeros((capacity, edge), jnp.float32)
    start = 0
    for g in range(group_total):
        for block in range(share):
            out_ref[g, block] = padded_ref[block, pl.ds(start, capacity), :]
        start = start + counts_ref[g]


def regroup(counts, rows, group_total, capacity):
    share, row_total, edge = rows.shape
    return pl.pallas_call(
        regroup_kernel,
        in_specs=[pl.BlockSpec(memory_space=pltpu.SMEM), pl.BlockSpec(memory_space=pltpu.VMEM)],
        out_specs=pl.BlockSpec(memory_space=pltpu.VMEM),
        out_shape=jax.ShapeDtypeStruct((group_total, share, capacity, edge), jnp.float32),
        scratch_shapes=[pltpu.VMEM((share, row_total + capacity, edge), jnp.float32)],
        compiler_params=pltpu.CompilerParams(vmem_limit_bytes=kernel_vmem),
        name="regroup",
    )(counts, rows)


def per_device(intensity, counts, segment_ids, tile_ids, block_order, tiles):
    row_total = intensity.shape[1]
    voxel_edge = tiles.shape[1]
    group_total = lax.axis_size("angle")
    tile_total = lax.axis_size("tile")
    group = lax.axis_index("angle")
    capacity = 2 * row_total // group_total
    share = block_order.shape[0] // (tile_total * group_total)
    assert group_total >= 4 and group_total & (group_total - 1) == 0

    def swap(values, partner):
        return lax.ppermute(values, "angle", [(i, i ^ partner) for i in range(group_total)])

    thickness = paganin_thickness(intensity, voxel_edge)
    sources = [thickness]
    for shift in range(1, tile_total):
        ring = [(i, (i + shift) % tile_total) for i in range(tile_total)]
        sources.append(lax.ppermute(thickness, "tile", ring))
    place = jnp.stack([group, lax.axis_index("tile"), jnp.int32(group_total)]).astype(jnp.int32)
    tables = (place, segment_ids, tile_ids, block_order, tiles, sources, share)
    half = group_total // 2
    far = list(range(half, group_total, 2))
    near = list(range(0, half, 2))
    far_odd, unscale = backproject([k + 1 for k in far], *tables)
    near_odd, _ = backproject([k + 1 for k in near], *tables)
    even, _ = backproject(far + near, *tables)
    far_sums = even[: len(far)] + swap(far_odd.astype(jnp.float16), 1).astype(jnp.float32)
    sent = far_sums.astype(jnp.float16)
    parts = [swap(sent[i], k) for i, k in enumerate(far)]
    near_odd = near_odd.astype(jnp.float16)
    near_odd, _ = lax.optimization_barrier((near_odd, sent))
    near_sums = even[len(far) :] + swap(near_odd, 1).astype(jnp.float32)
    parts += [swap(near_sums[i].astype(jnp.float16), k) for i, k in enumerate(near) if k]
    rows = near_sums[0]
    for part in parts:
        rows = rows + part.astype(jnp.float32)
    slots = regroup(counts, rows, group_total, capacity) * (1.0 / group_total)
    arrived = lax.all_to_all(slots.astype(jnp.float16), "angle", split_axis=0, concat_axis=0, tiled=True)
    arrived = arrived.reshape(group_total * share, capacity, voxel_edge)
    volume = arrived.astype(jnp.float32) * (unscale[0, 0] * group_total)
    slot_valid = jnp.arange(capacity, dtype=jnp.int32) < counts[group]
    volume = jnp.where(slot_valid[None, :, None], volume, 0.0)
    return jnp.swapaxes(volume, 0, 1)[None]


def solution(mesh):
    in_specs = (P(("groups", "angle", "tile"), None, None), P("groups"), P(), P(), P("groups"), P())
    out_specs = P(("groups", "angle"), None, "tile", None)
    return jax.shard_map(
        per_device, mesh=mesh, in_specs=in_specs, out_specs=out_specs, check_vma=False
    )
```

```python
import functools
import math

import jax
import jax.numpy as jnp
import numpy as np
from jax import lax
from jax.experimental import pallas as pl
from jax.experimental.pallas import tpu as pltpu
from jax.sharding import PartitionSpec as P

paganin_alpha = 2.0
lanes = 128
sublanes = 8
strands = 16
chunks = strands * sublanes
pitch_pad = 1
kernel_vmem = 24 << 20
thickness_bound = 1.75
send_bound = 60000.0


def split_parts(values):
    high = values.astype(jnp.bfloat16)
    low = (values - high.astype(jnp.float32)).astype(jnp.bfloat16)
    return high, low


def paired_parts(values):
    high, low = split_parts(values)
    return jnp.concatenate([high, low, high], axis=1)


def paired_table(matrix, axis):
    high = matrix.astype(jnp.bfloat16)
    low = (matrix - high.astype(np.float64)).astype(jnp.bfloat16)
    return jnp.asarray(np.concatenate([high, high, low], axis=axis))


def filter_tables(row_total, chunk):
    index = np.arange(row_total)
    phase = 2.0 * np.pi / row_total * (index[:, None] * index[None, :] % row_total)
    hartley = (np.cos(phase) + np.sin(phase)) / math.sqrt(row_total)
    row_weight = 4.0 * np.square(np.sin(np.pi * index / row_total))
    half = (1.0 + paganin_alpha * (row_weight + 2.0)) / (2.0 * paganin_alpha)
    root = half - np.sqrt(half * half - 1.0)
    levels = chunks.bit_length() - 1
    powers = [root] + [root ** (chunk << s) for s in range(levels)]
    powers.append(1.0 / (1.0 - root ** (chunk * chunks)))
    powers = np.repeat(np.stack(powers), sublanes, axis=0)
    step = np.arange(chunk)[:, None]
    ahead = root ** (step + 1) * (1.0 - root ** (2 * (chunk - step))) / (1.0 - root * root)
    behind = root ** (chunk - step)
    powers = np.concatenate([ahead, behind, powers], axis=0).astype(np.float32)
    back = hartley * (root / paganin_alpha)[None, :]
    return paired_table(hartley, 0), paired_table(back, 1), jnp.asarray(powers)


def chunk_shift(values, distance):
    moved = []
    for q in range(strands):
        turns, source = divmod(q - distance, strands)
        moved.append(pltpu.roll(values[source], -turns % sublanes, 0) if turns % sublanes else values[source])
    return moved


def carries(ends, powers_ref, first, direction):
    levels = chunks.bit_length() - 1
    for s in range(levels):
        power = powers_ref[pl.ds(first + s * sublanes, sublanes), :]
        before = chunk_shift(ends, direction << s)
        ends = [end + power * other for end, other in zip(ends, before)]
    whole = powers_ref[pl.ds(first + levels * sublanes, sublanes), :]
    return [whole * other for other in chunk_shift(ends, direction)]


def filter_kernel(
    forward_ref, back_ref, powers_ref, f_ref, out_ref, modes_ref, enter_ref, return_ref
):
    row_total, width = f_ref.shape[1:]
    edge = out_ref.shape[3]
    span = width // sublanes
    pitch = modes_ref.shape[0] // sublanes
    chunk = span // strands

    def place(column):
        return column // span * pitch + column % span

    for column in range(0, width, span):
        turned = [f_ref[0, :, start : start + lanes].T for start in range(column, column + span, lanes)]
        modes_ref[pl.ds(place(column), span), :] = jnp.dot(
            paired_parts(jnp.concatenate(turned, axis=0)), forward_ref[...], preferred_element_type=jnp.float32
        )

    root = powers_ref[pl.ds(2 * chunk, sublanes), :]
    first = 2 * chunk + sublanes

    def strand(q, step):
        return pl.ds(q * chunk + step, sublanes, stride=pitch)

    def sweep(order):
        values = [jnp.zeros((sublanes, row_total), jnp.float32)] * strands
        for step in order:
            for q in range(strands):
                values[q] = modes_ref[strand(q, step), :] + root * values[q]
                modes_ref[strand(q, step), :] = values[q]
        return values

    ends = sweep(range(chunk))
    firsts = sweep(range(chunk)[::-1])
    entering = carries(ends, powers_ref, first, 1)
    head = powers_ref[pl.ds(0, 1), :]
    firsts = [value + head * enter for value, enter in zip(firsts, entering)]
    returning = carries(firsts, powers_ref, first, -1)
    for q in range(strands):
        enter_ref[pl.ds(q, sublanes, stride=strands + pitch_pad), :] = entering[q]
        return_ref[pl.ds(q, sublanes, stride=strands + pitch_pad), :] = returning[q]

    def solved(column):
        pieces = []
        for start in range(column, column + span, chunk):
            rows = modes_ref[pl.ds(place(start), chunk), :]
            number = start // chunk + start // span * pitch_pad
            pieces.append(
                rows
                + powers_ref[pl.ds(0, chunk), :] * enter_ref[pl.ds(number, 1), :]
                + powers_ref[pl.ds(chunk, chunk), :] * return_ref[pl.ds(number, 1), :]
            )
        return jnp.concatenate(pieces, axis=0)

    for column in range(0, width, span):
        filtered = lax.dot_general(
            back_ref[...],
            paired_parts(solved(column)),
            (((1,), (1,)), ((), ())),
            preferred_element_type=jnp.float32,
        )
        thickness = (-jnp.log(filtered)).astype(jnp.bfloat16)
        for part in range(span // edge):
            out_ref[0, column // edge + part] = thickness[:, part * edge : (part + 1) * edge]


def paganin_thickness(intensity, voxel_edge):
    angle_count, row_total, width = intensity.shape
    assert row_total == lanes and width % (sublanes * lanes) == 0 and lanes % voxel_edge == 0
    forward, back, powers = filter_tables(row_total, width // chunks)
    segments = width // voxel_edge
    whole = lambda a: (0, 0)
    return pl.pallas_call(
        filter_kernel,
        grid=(angle_count,),
        in_specs=[
            pl.BlockSpec(forward.shape, whole),
            pl.BlockSpec(back.shape, whole),
            pl.BlockSpec(powers.shape, whole),
            pl.BlockSpec((1, row_total, width), lambda a: (a, 0, 0)),
        ],
        out_specs=pl.BlockSpec((1, segments, row_total, voxel_edge), lambda a: (a, 0, 0, 0)),
        out_shape=jax.ShapeDtypeStruct((angle_count, segments, row_total, voxel_edge), jnp.bfloat16),
        scratch_shapes=[
            pltpu.VMEM((width + sublanes * pitch_pad, row_total), jnp.float32),
            pltpu.VMEM((chunks + sublanes * pitch_pad, row_total), jnp.float32),
            pltpu.VMEM((chunks + sublanes * pitch_pad, row_total), jnp.float32),
        ],
        compiler_params=pltpu.CompilerParams(vmem_limit_bytes=kernel_vmem),
        name="paganin",
    )(*[pltpu.with_memory_space_constraint(v, pltpu.HBM) for v in (forward, back, powers, intensity)])


def send_scale(largest, angle_total, voxel_edge):
    limit = send_bound / (angle_total * voxel_edge * thickness_bound)
    scale = jnp.float32(1.0)
    for bits in (32, 16, 8, 4, 2, 1):
        wider = scale * float(2**bits)
        scale = jnp.where(largest * wider <= limit, wider, scale)
    return scale


def backproject_kernel(
    partners, place_ref, segment_ref, tile_ref, order_ref, tiles_ref, *refs
):
    *thickness_refs, out_ref, unscale_ref = refs
    chunk_total, share, row_total, edge = out_ref.shape
    source_total = len(thickness_refs)
    angle_count = thickness_refs[0].shape[0]
    group, tile, group_total = place_ref[0], place_ref[1], place_ref[2]
    largest = jnp.max(jnp.abs(tiles_ref[...].astype(jnp.float32)))
    scale = send_scale(largest, angle_count * source_total, edge)
    unscale_ref[...] = jnp.full(unscale_ref.shape, 1.0, jnp.float32) / scale

    for chunk, partner in enumerate(partners):
        owner = lax.bitwise_xor(group, jnp.int32(partner))
        for block in range(share):
            voxel_block = order_ref[(tile * group_total + owner) * share + block]
            pieces, matrices = [], []
            for shift, thickness_ref in enumerate(thickness_refs):
                source = lax.rem(tile + source_total - shift, source_total)
                for local in range(angle_count):
                    angle = (group * source_total + source) * angle_count + local
                    pieces.append(thickness_ref[local, segment_ref[angle, voxel_block]])
                    matrices.append(tiles_ref[tile_ref[angle, voxel_block]])
            total = jnp.dot(
                jnp.concatenate(pieces, axis=1),
                jnp.concatenate(matrices, axis=0),
                preferred_element_type=jnp.float32,
            )
            out_ref[chunk, block] = total * scale


def resident(values):
    return pltpu.with_memory_space_constraint(values, pltpu.VMEM)


def backproject(partners, place, segment_ids, tile_ids, block_order, tiles, thickness, share):
    row_total, edge = thickness[0].shape[2:]
    angle_total = thickness[0].shape[0] * len(thickness)
    blocks = len(partners) * share
    scalars = pl.BlockSpec(memory_space=pltpu.SMEM)
    vectors = pl.BlockSpec(memory_space=pltpu.VMEM)
    return pl.pallas_call(
        functools.partial(backproject_kernel, tuple(partners)),
        in_specs=[scalars] * 4 + [vectors] * (1 + len(thickness)),
        out_specs=[vectors, vectors],
        out_shape=[
            jax.ShapeDtypeStruct((len(partners), share, row_total, edge), jnp.float32),
            jax.ShapeDtypeStruct((8, edge), jnp.float32),
        ],
        cost_estimate=pl.CostEstimate(
            flops=2 * blocks * angle_total * row_total * edge * edge,
            bytes_accessed=4 * blocks * row_total * edge,
            transcendentals=0,
        ),
        compiler_params=pltpu.CompilerParams(vmem_limit_bytes=kernel_vmem),
        name="backproject",
    )(place, segment_ids, tile_ids, block_order, tiles, *[resident(t) for t in thickness])


def regroup_kernel(counts_ref, rows_ref, out_ref, padded_ref):
    group_total, share, capacity, edge = out_ref.shape
    row_total = rows_ref.shape[1]
    for block in range(share):
        padded_ref[block, :row_total] = rows_ref[block]
        padded_ref[block, row_total:] = jnp.zeros((capacity, edge), jnp.float32)
    start = 0
    for g in range(group_total):
        for block in range(share):
            out_ref[g, block] = padded_ref[block, pl.ds(start, capacity), :]
        start = start + counts_ref[g]


def regroup(counts, rows, group_total, capacity):
    share, row_total, edge = rows.shape
    return pl.pallas_call(
        regroup_kernel,
        in_specs=[pl.BlockSpec(memory_space=pltpu.SMEM), pl.BlockSpec(memory_space=pltpu.VMEM)],
        out_specs=pl.BlockSpec(memory_space=pltpu.VMEM),
        out_shape=jax.ShapeDtypeStruct((group_total, share, capacity, edge), jnp.float32),
        scratch_shapes=[pltpu.VMEM((share, row_total + capacity, edge), jnp.float32)],
        compiler_params=pltpu.CompilerParams(vmem_limit_bytes=kernel_vmem),
        name="regroup",
    )(counts, rows)


def per_device(intensity, counts, segment_ids, tile_ids, block_order, tiles):
    row_total = intensity.shape[1]
    voxel_edge = tiles.shape[1]
    group_total = lax.axis_size("angle")
    tile_total = lax.axis_size("tile")
    group = lax.axis_index("angle")
    capacity = 2 * row_total // group_total
    share = block_order.shape[0] // (tile_total * group_total)
    assert group_total >= 4 and group_total & (group_total - 1) == 0

    def swap(values, partner):
        return lax.ppermute(values, "angle", [(i, i ^ partner) for i in range(group_total)])

    thickness = paganin_thickness(intensity, voxel_edge)
    sources = [thickness]
    for shift in range(1, tile_total):
        ring = [(i, (i + shift) % tile_total) for i in range(tile_total)]
        sources.append(lax.ppermute(thickness, "tile", ring))
    place = jnp.stack([group, lax.axis_index("tile"), jnp.int32(group_total)]).astype(jnp.int32)
    tables = (place, segment_ids, tile_ids, block_order, tiles, sources, share)
    half = group_total // 2
    far = list(range(half, group_total, 2))
    near = list(range(0, half, 2))
    far_odd, unscale = backproject([k + 1 for k in far], *tables)
    near_odd, _ = backproject([k + 1 for k in near], *tables)
    even, _ = backproject(far + near, *tables)
    far_sums = even[: len(far)] + swap(far_odd.astype(jnp.float16), 1).astype(jnp.float32)
    sent = far_sums.astype(jnp.float16)
    parts = [swap(sent[i], k) for i, k in enumerate(far)]
    near_odd = near_odd.astype(jnp.float16)
    near_odd, _ = lax.optimization_barrier((near_odd, sent))
    near_sums = even[len(far) :] + swap(near_odd, 1).astype(jnp.float32)
    parts += [swap(near_sums[i].astype(jnp.float16), k) for i, k in enumerate(near) if k]
    rows = near_sums[0]
    for part in parts:
        rows = rows + part.astype(jnp.float32)
    slots = regroup(counts, rows, group_total, capacity) * (1.0 / group_total)
    arrived = lax.all_to_all(slots.astype(jnp.float16), "angle", split_axis=0, concat_axis=0, tiled=True)
    arrived = arrived.reshape(group_total * share, capacity, voxel_edge)
    volume = arrived.astype(jnp.float32) * (unscale[0, 0] * group_total)
    slot_valid = jnp.arange(capacity, dtype=jnp.int32) < counts[group]
    volume = jnp.where(slot_valid[None, :, None], volume, 0.0)
    return jnp.swapaxes(volume, 0, 1)[None]


def solution(mesh):
    in_specs = (P(("groups", "angle", "tile"), None, None), P("groups"), P(), P(), P("groups"), P())
    out_specs = P(("groups", "angle"), None, "tile", None)
    return jax.shard_map(
        per_device, mesh=mesh, in_specs=in_specs, out_specs=out_specs, check_vma=False
    )
```

```python
import functools
import math

import jax
import jax.numpy as jnp
import numpy as np
from jax import lax
from jax.experimental import pallas as pl
from jax.experimental.pallas import tpu as pltpu
from jax.sharding import PartitionSpec as P


paganin_alpha = 2.0
lanes = 128
sublanes = 8
strands = 16
chunks = strands * sublanes
pitch_pad = 1
kernel_vmem = 24 << 20
thickness_bound = 1.75
send_bound = 60000.0


def split_parts(values):
    high = values.astype(jnp.bfloat16)
    low = (values - high.astype(jnp.float32)).astype(jnp.bfloat16)
    return high, low


def paired_parts(values):
    high, low = split_parts(values)
    return jnp.concatenate([high, low, high], axis=1)


def paired_table(matrix, axis):
    high = matrix.astype(jnp.bfloat16)
    low = (matrix - high.astype(np.float64)).astype(jnp.bfloat16)
    return jnp.asarray(np.concatenate([high, high, low], axis=axis))


def filter_tables(row_total, chunk):
    index = np.arange(row_total)
    phase = 2.0 * np.pi / row_total * (index[:, None] * index[None, :] % row_total)
    hartley = (np.cos(phase) + np.sin(phase)) / math.sqrt(row_total)
    row_weight = 4.0 * np.square(np.sin(np.pi * index / row_total))
    half = (1.0 + paganin_alpha * (row_weight + 2.0)) / (2.0 * paganin_alpha)
    root = half - np.sqrt(half * half - 1.0)
    levels = chunks.bit_length() - 1
    powers = [root] + [root ** (chunk << s) for s in range(levels)]
    powers.append(1.0 / (1.0 - root ** (chunk * chunks)))
    powers = np.repeat(np.stack(powers), sublanes, axis=0)
    step = np.arange(chunk)[:, None]
    ahead = root ** (step + 1) * (1.0 - root ** (2 * (chunk - step))) / (1.0 - root * root)
    behind = root ** (chunk - step)
    powers = np.concatenate([ahead, behind, powers], axis=0).astype(np.float32)
    back = hartley * (root / paganin_alpha)[None, :]
    return paired_table(hartley, 0), paired_table(back, 1), jnp.asarray(powers)


def chunk_shift(values, distance):
    moved = []
    for q in range(strands):
        turns, source = divmod(q - distance, strands)
        moved.append(pltpu.roll(values[source], -turns % sublanes, 0) if turns % sublanes else values[source])
    return moved


def carries(ends, powers_ref, first, direction):
    levels = chunks.bit_length() - 1
    for s in range(levels):
        power = powers_ref[pl.ds(first + s * sublanes, sublanes), :]
        before = chunk_shift(ends, direction << s)
        ends = [end + power * other for end, other in zip(ends, before)]
    whole = powers_ref[pl.ds(first + levels * sublanes, sublanes), :]
    return [whole * other for other in chunk_shift(ends, direction)]


def filter_kernel(
    forward_ref, back_ref, powers_ref, f_ref, out_ref, modes_ref, enter_ref, return_ref
):
    row_total, width = f_ref.shape[1:]
    edge = out_ref.shape[3]
    span = width // sublanes
    pitch = modes_ref.shape[0] // sublanes
    chunk = span // strands

    def place(column):
        return column // span * pitch + column % span

    for column in range(0, width, span):
        turned = [f_ref[0, :, start : start + lanes].T for start in range(column, column + span, lanes)]
        modes_ref[pl.ds(place(column), span), :] = jnp.dot(
            paired_parts(jnp.concatenate(turned, axis=0)), forward_ref[...], preferred_element_type=jnp.float32
        )

    root = powers_ref[pl.ds(2 * chunk, sublanes), :]
    first = 2 * chunk + sublanes

    def strand(q, step):
        return pl.ds(q * chunk + step, sublanes, stride=pitch)

    def sweep(order):
        values = [jnp.zeros((sublanes, row_total), jnp.float32)] * strands
        for step in order:
            for q in range(strands):
                values[q] = modes_ref[strand(q, step), :] + root * values[q]
                modes_ref[strand(q, step), :] = values[q]
        return values

    ends = sweep(range(chunk))
    firsts = sweep(range(chunk)[::-1])
    entering = carries(ends, powers_ref, first, 1)
    head = powers_ref[pl.ds(0, 1), :]
    firsts = [value + head * enter for value, enter in zip(firsts, entering)]
    returning = carries(firsts, powers_ref, first, -1)
    for q in range(strands):
        enter_ref[pl.ds(q, sublanes, stride=strands + pitch_pad), :] = entering[q]
        return_ref[pl.ds(q, sublanes, stride=strands + pitch_pad), :] = returning[q]

    def solved(column):
        pieces = []
        for start in range(column, column + span, chunk):
            rows = modes_ref[pl.ds(place(start), chunk), :]
            number = start // chunk + start // span * pitch_pad
            pieces.append(
                rows
                + powers_ref[pl.ds(0, chunk), :] * enter_ref[pl.ds(number, 1), :]
                + powers_ref[pl.ds(chunk, chunk), :] * return_ref[pl.ds(number, 1), :]
            )
        return jnp.concatenate(pieces, axis=0)

    for column in range(0, width, span):
        filtered = lax.dot_general(
            back_ref[...],
            paired_parts(solved(column)),
            (((1,), (1,)), ((), ())),
            preferred_element_type=jnp.float32,
        )
        thickness = (-jnp.log(filtered)).astype(jnp.bfloat16)
        for part in range(span // edge):
            out_ref[0, column // edge + part] = thickness[:, part * edge : (part + 1) * edge]


def paganin_thickness(intensity, voxel_edge):
    angle_count, row_total, width = intensity.shape
    assert row_total == lanes and width % (sublanes * lanes) == 0 and lanes % voxel_edge == 0
    forward, back, powers = filter_tables(row_total, width // chunks)
    segments = width // voxel_edge
    whole = lambda a: (0, 0)
    return pl.pallas_call(
        filter_kernel,
        grid=(angle_count,),
        in_specs=[
            pl.BlockSpec(forward.shape, whole),
            pl.BlockSpec(back.shape, whole),
            pl.BlockSpec(powers.shape, whole),
            pl.BlockSpec((1, row_total, width), lambda a: (a, 0, 0)),
        ],
        out_specs=pl.BlockSpec((1, segments, row_total, voxel_edge), lambda a: (a, 0, 0, 0)),
        out_shape=jax.ShapeDtypeStruct((angle_count, segments, row_total, voxel_edge), jnp.bfloat16),
        scratch_shapes=[
            pltpu.VMEM((width + sublanes * pitch_pad, row_total), jnp.float32),
            pltpu.VMEM((chunks + sublanes * pitch_pad, row_total), jnp.float32),
            pltpu.VMEM((chunks + sublanes * pitch_pad, row_total), jnp.float32),
        ],
        compiler_params=pltpu.CompilerParams(vmem_limit_bytes=kernel_vmem),
        name="paganin",
    )(*[pltpu.with_memory_space_constraint(v, pltpu.HBM) for v in (forward, back, powers, intensity)])


def send_scale(largest, angle_total, voxel_edge):
    limit = send_bound / (angle_total * voxel_edge * thickness_bound)
    scale = jnp.float32(1.0)
    for bits in (32, 16, 8, 4, 2, 1):
        wider = scale * float(2**bits)
        scale = jnp.where(largest * wider <= limit, wider, scale)
    return scale


def backproject_kernel(
    partners, place_ref, order_ref, segment_all, tile_all, tiles_ref, thickness_ref, *refs
):
    *out_refs, unscale_ref, segment_ref, tile_ref, arrival = refs
    _, share, _, edge = out_refs[0].shape
    tile_total = len(out_refs)
    angle_count = thickness_ref.shape[0]
    group, tile, group_total = place_ref[0], place_ref[1], place_ref[2]
    chip_angles = segment_ref.shape[0]
    chip_rows = pl.ds(pl.multiple_of(group * chip_angles, chip_angles), chip_angles)
    copies = [
        pltpu.make_async_copy(segment_all.at[chip_rows], segment_ref, arrival.at[0]),
        pltpu.make_async_copy(tile_all.at[chip_rows], tile_ref, arrival.at[1]),
    ]
    for copy in copies:
        copy.start()
    largest = jnp.max(jnp.abs(tiles_ref[...].astype(jnp.float32)))
    scale = send_scale(largest, angle_count * tile_total, edge)
    unscale_ref[...] = jnp.full(unscale_ref.shape, 1.0, jnp.float32) / scale
    for copy in copies:
        copy.wait()

    for chunk, partner in enumerate(partners):
        owner = lax.bitwise_xor(group, jnp.int32(partner))
        for shift, out_ref in enumerate(out_refs):
            target = lax.rem(tile + shift, tile_total)
            for block in range(share):
                voxel_block = order_ref[(target * group_total + owner) * share + block]
                pieces, matrices = [], []
                for local in range(angle_count):
                    angle = tile * angle_count + local
                    pieces.append(thickness_ref[local, segment_ref[angle, voxel_block]])
                    matrices.append(tiles_ref[tile_ref[angle, voxel_block]])
                total = jnp.dot(
                    jnp.concatenate(pieces, axis=1),
                    jnp.concatenate(matrices, axis=0),
                    preferred_element_type=jnp.float32,
                )
                out_ref[chunk, block] = total * scale


def backproject(partners, place, segment_ids, tile_ids, block_order, tiles, thickness, share, tile_total):
    angle_count, _, row_total, edge = thickness.shape
    shape = (len(partners), share, row_total, edge)
    blocks = len(partners) * share * tile_total
    scalars = pl.BlockSpec(memory_space=pltpu.SMEM)
    vectors = pl.BlockSpec(memory_space=pltpu.VMEM)
    return pl.pallas_call(
        functools.partial(backproject_kernel, tuple(partners)),
        in_specs=[scalars] * 2 + [pl.BlockSpec(memory_space=pl.ANY)] * 2 + [vectors] * 2,
        out_specs=[vectors] * (tile_total + 1),
        scratch_shapes=[
            pltpu.SMEM((angle_count * tile_total, segment_ids.shape[1]), jnp.int32),
            pltpu.SMEM((angle_count * tile_total, segment_ids.shape[1]), jnp.int32),
            pltpu.SemaphoreType.DMA((2,)),
        ],
        out_shape=[jax.ShapeDtypeStruct(shape, jnp.float32)] * tile_total
        + [jax.ShapeDtypeStruct((8, edge), jnp.float32)],
        cost_estimate=pl.CostEstimate(
            flops=2 * blocks * angle_count * row_total * edge * edge,
            bytes_accessed=4 * blocks * row_total * edge,
            transcendentals=0,
        ),
        compiler_params=pltpu.CompilerParams(vmem_limit_bytes=kernel_vmem),
        name="backproject",
    )(place, block_order, segment_ids, tile_ids, tiles, pltpu.with_memory_space_constraint(thickness, pltpu.VMEM))


def regroup_kernel(counts_ref, rows_ref, out_ref, padded_ref):
    group_total, share, capacity, edge = out_ref.shape
    row_total = rows_ref.shape[1]
    for block in range(share):
        padded_ref[block, :row_total] = rows_ref[block]
        padded_ref[block, row_total:] = jnp.zeros((capacity, edge), jnp.float32)
    start = 0
    for g in range(group_total):
        for block in range(share):
            out_ref[g, block] = padded_ref[block, pl.ds(start, capacity), :]
        start = start + counts_ref[g]


def regroup(counts, rows, group_total, capacity):
    share, row_total, edge = rows.shape
    return pl.pallas_call(
        regroup_kernel,
        in_specs=[pl.BlockSpec(memory_space=pltpu.SMEM), pl.BlockSpec(memory_space=pltpu.VMEM)],
        out_specs=pl.BlockSpec(memory_space=pltpu.VMEM),
        out_shape=jax.ShapeDtypeStruct((group_total, share, capacity, edge), jnp.float32),
        scratch_shapes=[pltpu.VMEM((share, row_total + capacity, edge), jnp.float32)],
        compiler_params=pltpu.CompilerParams(vmem_limit_bytes=kernel_vmem),
        name="regroup",
    )(counts, rows)


def per_device(intensity, counts, segment_ids, tile_ids, block_order, tiles):
    row_total = intensity.shape[1]
    voxel_edge = tiles.shape[1]
    group_total = lax.axis_size("angle")
    tile_total = lax.axis_size("tile")
    group = lax.axis_index("angle")
    capacity = 2 * row_total // group_total
    share = block_order.shape[0] // (tile_total * group_total)
    assert group_total >= 4 and group_total & (group_total - 1) == 0

    def swap(values, partner):
        return lax.ppermute(values, "angle", [(i, i ^ partner) for i in range(group_total)])

    def chip_sums(partners, place):
        own, *others, unscale = backproject(
            partners, place, segment_ids, tile_ids, block_order, tiles, thickness, share, tile_total
        )
        for shift, other in enumerate(others, 1):
            ring = [(i, (i + shift) % tile_total) for i in range(tile_total)]
            own = own + lax.ppermute(other.astype(jnp.float16), "tile", ring).astype(jnp.float32)
        return own, unscale

    thickness = paganin_thickness(intensity, voxel_edge)
    place = jnp.stack([group, lax.axis_index("tile"), jnp.int32(group_total)]).astype(jnp.int32)
    half = group_total // 2
    far = list(range(half, group_total, 2))
    quarter = half // 2
    first, unscale = chip_sums([k + 1 for k in far] + list(range(quarter, half)), place)
    first = first.astype(jnp.float16)
    place, _ = lax.optimization_barrier((place, first))
    rest, _ = chip_sums(far + list(range(quarter)), place)
    folded = swap(first[: len(far)], 1)
    sent = (rest[: len(far)] + folded.astype(jnp.float32)).astype(jnp.float16)
    parts = [swap(sent[i], far[i]) for i in range(len(far))[::-1]]
    settled = swap(first[len(far) :], quarter)
    settled, _ = lax.optimization_barrier((settled, sent))
    near_sums = rest[len(far) :] + settled.astype(jnp.float32)
    parts += [swap(near_sums[k].astype(jnp.float16), k) for k in range(1, quarter)]
    rows = near_sums[0]
    for part in parts:
        rows = rows + part.astype(jnp.float32)
    slots = regroup(counts, rows, group_total, capacity) * (1.0 / group_total)
    arrived = lax.all_to_all(slots.astype(jnp.float16), "angle", split_axis=0, concat_axis=0, tiled=True)
    arrived = arrived.reshape(group_total * share, capacity, voxel_edge)
    volume = arrived.astype(jnp.float32) * (unscale[0, 0] * group_total)
    slot_valid = jnp.arange(capacity, dtype=jnp.int32) < counts[group]
    volume = jnp.where(slot_valid[None, :, None], volume, 0.0)
    return jnp.swapaxes(volume, 0, 1)[None]


def solution(mesh):
    in_specs = (P(("groups", "angle", "tile"), None, None), P("groups"), P(), P(), P("groups"), P())
    out_specs = P(("groups", "angle"), None, "tile", None)
    return jax.shard_map(per_device, mesh=mesh, in_specs=in_specs, out_specs=out_specs, check_vma=False)
```
